32 devices in a mesh: col: 8 (over y, x, core), row: 4 (over z).
Axes of the slice: x: 2, y: 2, z: 4, core: 2. Of those that a mesh axis runs over, the one named last changes fastest.
Arguments:
- samples_x: bfloat16 [512, 98304], P('row', 'col'), may hold values from -6 to 6
- targets: bfloat16 [512, 98304], P('row', 'col'), may hold values from -6 to 6
- times: int32 [512], P('row'), may hold values from 0 to 63
- block_rows: int32 [576], P(('col', 'row')), may hold values from 0 to 767, as said below
- block_cols: int32 [576], P(('col', 'row')), may hold values from 0 to 767, as said below
Outputs:
- coeffs: float32 [576, 128, 128], P(('col', 'row'))
- residual: float32 [512, 98304], P('row', 'col')
The draws below stay inside these ranges and needn't reach their ends.
Inputs may be any that keep to these rules, and one draw needn't show every extreme that they name: `block_rows`: the blocks are listed by column group (the 96 column blocks c * 96 to (c + 1) * 96 - 1 form group c), and within a group in 8 runs of 9 blocks, run g holding row blocks of group g; no block appears twice. `block_cols`: each block's column block lies in the group of its place in the list, as described for block_rows.
All inputs are finite; a program needn't handle non-finite values.
Results may differ from the reference program's by a relative error of at most 0.009.
Values may be sent and summed in bfloat16 or wider, within the bound.
A program may use at most 192 MiB of HBM per device.

```python
import jax
import jax.numpy as jnp
from jax import lax

TAXA = 98304
BLOCK = 128
RUN = 9
SAMP_ROW = 128
ITERS = 2
T_STEPS = 64
CBLK = 96
BLOCKS = 576
SAMPLES = 512
N_COL = 8
N_ROW = 4


def pattern_pairs(key):
    keys = jax.random.split(jax.random.fold_in(key, 11), N_COL * N_COL)

    def one_run(run_key):
        return jax.random.permutation(run_key, CBLK * CBLK)[:RUN].astype(jnp.int32)
    picks = jax.vmap(one_run)(keys)
    grid = jnp.arange(N_COL * N_COL, dtype=jnp.int32)
    col_group = grid // N_COL
    src_group = grid % N_COL
    rows = src_group[:, None] * CBLK + picks // CBLK
    cols = col_group[:, None] * CBLK + picks % CBLK
    return (rows.reshape(-1).astype(jnp.int32), cols.reshape(-1).astype(jnp.int32))


def draw_block_rows(key, part):
    rows, cols = pattern_pairs(key)
    return rows


def draw_block_cols(key, part):
    rows, cols = pattern_pairs(key)
    return cols


def place_ends(entries, stream_key, low, high):
    dims = entries.shape
    place = [jax.random.randint(jax.random.fold_in(stream_key, axis), (), 0, dims[axis]) for axis in range(len(dims))]
    entries = entries.at[tuple(place)].set(low)
    longest = dims.index(max(dims))
    place[longest] = (place[longest] + 1) % dims[longest]
    return entries.at[tuple(place)].set(high)


def shard_levels(key, extent, cuts, least, top_value):
    level, own = 1.0, jax.random.fold_in(key, 6)
    for position, parts in cuts:
        heights = jnp.exp(jax.random.uniform(jax.random.fold_in(own, position), (parts,), jnp.float32, least / len(cuts), top_value / len(cuts)))
        level = level * jnp.repeat(heights, extent[position] // parts).reshape([-1 if axis == position else 1 for axis in range(len(extent))])
    return level


def noise(own_key, extent, scale, reach, cuts=(), kind=jnp.bfloat16):
    drawn = jax.random.normal(own_key, extent, jnp.float32) * scale
    if len(cuts) > 0:
        drawn = shard_levels(own_key, extent, cuts, -0.22, 0.18) * drawn
    return jnp.clip(drawn, min=-reach, max=reach).astype(kind)


def setup_inputs(seed: int = 0) -> dict:
    streams_of = jax.random.split(jax.random.key(seed), 6)
    samples_x = noise(streams_of[0], (SAMPLES, TAXA), 1.0, 6.0, ((0, 4), (1, 8)))
    targets = noise(streams_of[1], (SAMPLES, TAXA), 1.0, 6.0, ((0, 4), (1, 8)))
    times = place_ends(jax.random.randint(streams_of[2], (SAMPLES,), 0, T_STEPS), jax.random.fold_in(streams_of[2], 1), 0, T_STEPS - 1).astype(jnp.int32)
    block_rows = draw_block_rows(jax.random.fold_in(streams_of[5], 71), 0)
    block_cols = draw_block_cols(jax.random.fold_in(streams_of[5], 71), 0)
    return dict(samples_x=samples_x, targets=targets, times=times, block_rows=block_rows, block_cols=block_cols)


RIDGE_SHARE = 0.2


def reference(samples_x, targets, times, block_rows, block_cols):
    weight = (0.5 + times.astype(jnp.float32) / T_STEPS)[:, None]
    ridge = RIDGE_SHARE * SAMPLES
    block_count = TAXA // BLOCK
    x_blocks = samples_x.reshape(SAMPLES, block_count, BLOCK)
    x_groups = samples_x.reshape(N_ROW, SAMP_ROW, block_count, BLOCK)

    def adjoint(weighted):
        e_groups = weighted.reshape(N_ROW, SAMP_ROW, block_count, BLOCK)

        def one_group(total, pair):
            x_group, e_group = pair
            x_sel = jnp.take(x_group, block_rows, axis=1).astype(jnp.float32)
            e_sel = jnp.take(e_group, block_cols, axis=1).astype(jnp.float32)
            term = jnp.einsum("ska,skb->kab", x_sel, e_sel)
            rounded = lax.optimization_barrier(term.astype(jnp.bfloat16))
            return total + rounded.astype(jnp.float32), None

        start_total = jnp.zeros((BLOCKS, BLOCK, BLOCK), jnp.float32)
        total, unused = lax.scan(one_group, start_total, (x_groups, e_groups))
        return total

    def apply(direction):
        x_sel = jnp.take(x_blocks, block_rows, axis=1).astype(jnp.float32)
        contrib = jnp.einsum("ska,kab->skb", x_sel, direction.astype(jnp.float32))
        image = jnp.zeros((SAMPLES, block_count, BLOCK), jnp.float32).at[:, block_cols].add(contrib)
        return image.reshape(SAMPLES, TAXA)

    start = (targets.astype(jnp.float32) * weight).astype(jnp.bfloat16)
    gradient = adjoint(start)
    gamma = jnp.sum(gradient * gradient)
    direction = gradient.astype(jnp.bfloat16)
    coeffs = jnp.zeros((BLOCKS, BLOCK, BLOCK), jnp.float32)
    residual = targets.astype(jnp.float32)
    for step in range(ITERS):
        image = apply(direction)
        flat = direction.astype(jnp.float32)
        alpha = gamma / (jnp.sum(weight * image * image) + ridge * jnp.sum(flat * flat))
        coeffs = coeffs + alpha * flat
        residual = residual - alpha * image
        if step + 1 < ITERS:
            gradient = adjoint((residual * weight).astype(jnp.bfloat16)) - ridge * coeffs
            gamma_next = jnp.sum(gradient * gradient)
            direction = (gradient + (gamma_next / gamma) * flat).astype(jnp.bfloat16)
            gamma = gamma_next
    return coeffs, residual
```

```python
import functools

import jax
import jax.numpy as jnp
from jax import lax
from jax.experimental import pallas as pl
from jax.experimental.pallas import tpu as pltpu
from jax.sharding import PartitionSpec as P

BLOCK = 128
T_STEPS = 64
RIDGE_SHARE = 0.2
LANES = 128
SIZE = 3
LEAD = 4
FAR = 6
LATE = 2
VMEM = pltpu.VMEM
F32 = jnp.float32
BF16 = jnp.bfloat16
WHOLE = pl.BlockSpec(memory_space=pltpu.VMEM)
SCALARS = pl.BlockSpec(memory_space=pltpu.SMEM)
MESH = pl.DeviceIdType.MESH


def enter(axes):
    barrier = pltpu.get_barrier_semaphore()
    count = 0
    for axis in axes:
        n = lax.axis_size(axis)
        me = lax.axis_index(axis)
        for k in range(1, n):
            pl.semaphore_signal(
                barrier, inc=1, device_id={axis: lax.rem(me + k, n)}, device_id_type=MESH,
            )
        count += n - 1
    pl.semaphore_wait(barrier, count)


def push(src, dst, send, recv, axis, k):
    n = lax.axis_size(axis)
    return pltpu.make_async_remote_copy(
        src_ref=src, dst_ref=dst, send_sem=send, recv_sem=recv,
        device_id={axis: lax.rem(lax.axis_index(axis) + k, n)},
        device_id_type=MESH,
    )


def gather_small_kernel(x_ref, out_ref, send_c, recv_c, send_r, recv_r):
    cols, rows = lax.axis_size("col"), lax.axis_size("row")
    my_col, my_row = lax.axis_index("col"), lax.axis_index("row")
    enter(("col", "row"))
    out_ref[my_row, my_col] = x_ref[...]
    first = [
        push(x_ref, out_ref.at[my_row, my_col], send_c.at[k - 1], recv_c.at[k - 1], "col", k)
        for k in range(1, cols)
    ]
    for copy in first:
        copy.start()
    for copy in first:
        copy.wait()
    second = [
        push(out_ref.at[my_row], out_ref.at[my_row], send_r.at[k - 1], recv_r.at[k - 1], "row", k)
        for k in range(1, rows)
    ]
    for copy in second:
        copy.start()
    for copy in second:
        copy.wait()


def gather_small(x, call_id):
    cols, rows = lax.axis_size("col"), lax.axis_size("row")
    return pl.pallas_call(
        gather_small_kernel,
        out_shape=jax.ShapeDtypeStruct((rows, cols) + x.shape, x.dtype),
        in_specs=[WHOLE],
        out_specs=WHOLE,
        scratch_shapes=[
            pltpu.SemaphoreType.DMA((cols - 1,)), pltpu.SemaphoreType.DMA((cols - 1,)),
            pltpu.SemaphoreType.DMA((rows - 1,)), pltpu.SemaphoreType.DMA((rows - 1,)),
        ],
        compiler_params=pltpu.CompilerParams(collective_id=call_id, has_side_effects=True),
    )(x)


def block_dot(x, e):
    return lax.dot_general(x, e, (((0,), (0,)), ((), ())), preferred_element_type=F32)


def fold(values):
    return jnp.sum(values.reshape(values.shape[0] // 8, 8, BLOCK), axis=0)


def xor(a, b, bits):
    out = 0
    for i in range(bits):
        x = lax.rem(lax.div(a, 2 ** i), 2)
        if isinstance(b, int):
            y = (b >> i) & 1
        else:
            y = lax.rem(lax.div(b, 2 ** i), 2)
        out = out + (x + y - 2 * x * y) * 2 ** i
    return out


def fit_kernel(
    run, ridge, index_ref, ends_ref, x_ref, t_ref, w_ref, image_ref, coeffs_ref,
    give, x_all, near_sum, far_sum, arrived, d_ref, low_ref, s_ref, acc, scal, mine, by_col, line, by_row,
    send_x, recv_x, send_z, recv_z, send_c, recv_c, send_r, recv_r, credit,
):
    cols, rows = lax.axis_size("col"), lax.axis_size("row")
    my_col, my_row = lax.axis_index("col"), lax.axis_index("row")
    bits = (cols - 1).bit_length()
    count = x_all.shape[0]
    pieces = count // SIZE
    per_run = run // SIZE
    enter(("col", "row"))

    def select(s, target):
        base = xor(my_col, s, bits) * run

        def one(i, carry):
            column = index_ref[0, base + i] * BLOCK
            target[s * run + i] = x_ref[:, pl.ds(column, BLOCK)]
            return carry

        lax.fori_loop(0, run, one, 0, unroll=3)

    def exchange(s):
        place = pl.ds(s * run, run)
        return pltpu.make_async_remote_copy(
            src_ref=give.at[place], dst_ref=x_all.at[place],
            send_sem=send_x.at[s - 1], recv_sem=recv_x.at[s - 1],
            device_id={"col": xor(my_col, s, bits)}, device_id_type=MESH,
        )

    for s in range(1, cols):
        select(s, give)
        exchange(s).start()
    select(0, x_all)

    near = lax.div(2 * my_row, rows)
    far = 1 - near
    has_near = jnp.logical_and(my_row > 0, my_row < rows - 1)
    at_end = (my_row == 0) | (my_row == rows - 1)
    to_far = my_row + 1 - 2 * near
    to_near = my_row - 1 + 2 * near

    def forth(p):
        place = pl.ds(p * SIZE, SIZE)
        return pltpu.make_async_remote_copy(
            src_ref=near_sum.at[place], dst_ref=arrived.at[near, place],
            send_sem=send_z.at[near, p], recv_sem=recv_z.at[near, p],
            device_id={"row": to_far}, device_id_type=MESH,
        )

    def back(p):
        place = pl.ds(p * SIZE, SIZE)
        return pltpu.make_async_remote_copy(
            src_ref=far_sum.at[place], dst_ref=arrived.at[far, place],
            send_sem=send_z.at[far, p], recv_sem=recv_z.at[far, p],
            device_id={"row": to_near}, device_id_type=MESH,
        )

    def listed(p):
        s = lax.div(p, per_run)
        return xor(my_col, s, bits) * run + (p - s * per_run) * SIZE

    def store_terms(p, terms):
        for j in range(SIZE):
            near_sum[p * SIZE + j] = terms[j]
            far_sum[p * SIZE + j] = terms[j]
        pl.when(at_end)(lambda: forth(p).start())

    def pass_forth(p):
        forth(p).wait_recv()
        for j in range(SIZE):
            b = p * SIZE + j
            near_sum[b] = (far_sum[b].astype(F32) + arrived[near, b].astype(F32)).astype(BF16)
        forth(p).start()

    def pass_back(p):
        back(p).wait_recv()

        @pl.when(has_near)
        def _():
            for j in range(SIZE):
                b = p * SIZE + j
                far_sum[b] = (far_sum[b].astype(F32) + arrived[far, b].astype(F32)).astype(BF16)
            back(p).start()

    def sweep(make, settle, hooks, last):
        def body(q, carry):
            pl.when(q < pieces)(lambda: make(q))
            pl.when(has_near & (q >= LEAD) & (q < pieces + LEAD))(lambda: pass_forth(q - LEAD))
            pl.when((q >= FAR) & (q < pieces + FAR))(lambda: pass_back(q - FAR))
            for when, hook in hooks:
                pl.when(q == when)(hook)
            pl.when(q >= last)(lambda: settle(q - last))
            return carry

        lax.fori_loop(0, pieces + last, body, 0)

        def drain(p, carry):
            forth(p).wait_send()
            pl.when(has_near)(lambda: back(p).wait_send())
            return carry

        lax.fori_loop(0, pieces, drain, 0)

    def over_col(a, k):
        return push(mine.at[a], by_col.at[a, my_col], send_c.at[a, k - 1], recv_c.at[a, k - 1], "col", k)

    def over_row(a, k):
        return push(line.at[a], by_row.at[a, my_row], send_r.at[a, k - 1], recv_r.at[a, k - 1], "row", k)

    def reduce_start(a, wanted):
        tile = jnp.concatenate(
            [jnp.sum(acc[j], axis=0, keepdims=True) for j in wanted]
            + [jnp.zeros((8 - len(wanted), LANES), F32)], axis=0,
        )
        mine[a] = tile
        by_col[a, my_col] = tile
        for k in range(1, cols):
            over_col(a, k).start()

    def reduce_middle(a):
        for k in range(1, cols):
            over_col(a, k).wait()
        tile = by_col[a, 0]
        for j in range(1, cols):
            tile = tile + by_col[a, j]
        line[a] = tile
        by_row[a, my_row] = tile
        for k in range(1, rows):
            over_row(a, k).start()

    def reduce_end(a):
        for k in range(1, rows):
            over_row(a, k).wait()
        tile = by_row[a, 0]
        for j in range(1, rows):
            tile = tile + by_row[a, j]
        return jnp.sum(tile, axis=1, keepdims=True)

    def wide(value):
        return jnp.broadcast_to(value, (1, LANES))

    acc[...] = jnp.zeros_like(acc)
    s_ref[count] = jnp.zeros((BLOCK, BLOCK), F32)
    image_ref[count] = jnp.zeros((BLOCK, BLOCK), F32)

    def first_make(p):
        s = lax.div(p, per_run)

        @pl.when((s > 0) & (s * per_run == p))
        def _():
            place = pl.ds(s * run, run)
            pltpu.make_async_remote_copy(
                src_ref=give.at[place], dst_ref=x_all.at[place],
                send_sem=send_x.at[s - 1], recv_sem=recv_x.at[s - 1],
                device_id={"col": xor(my_col, s, bits)}, device_id_type=MESH,
            ).wait_recv()

        base = listed(p)
        terms = []
        for j in range(SIZE):
            place = pl.ds(index_ref[1, base + j] * BLOCK, BLOCK)
            e = (t_ref[:, place].astype(F32) * w_ref[...]).astype(BF16)
            terms.append(block_dot(x_all[p * SIZE + j], e).astype(BF16))
        store_terms(p, terms)

    def first_settle(p):
        base = listed(p)
        made = []
        for j in range(SIZE):
            b = p * SIZE + j
            total = near_sum[b].astype(F32) + arrived[far, b].astype(F32)
            rounded = total.astype(BF16)
            flat = rounded.astype(F32)
            d_ref[b] = rounded
            low_ref[b] = (total - flat).astype(BF16)
            made.append(jnp.dot(x_all[b], rounded, preferred_element_type=F32))
            acc[0] += fold(total * total)
            acc[1] += fold(flat * flat)
        for j in range(SIZE):
            b = p * SIZE + j
            image = made[j] + s_ref[index_ref[2, base + j]]
            s_ref[b] = image
            acc[2] += ends_ref[base + j] * fold(w_ref[...] * image * image)

    sweep(first_make, first_settle, [], FAR)
    for s in range(1, cols):
        exchange(s).wait_send()

    def greet(other):
        pl.semaphore_signal(credit, inc=1, device_id={"row": other}, device_id_type=MESH)

    has_left, has_right = my_row > 0, my_row < rows - 1
    pl.when(has_left)(lambda: greet(my_row - 1))
    pl.when(has_right)(lambda: greet(my_row + 1))
    reduce_start(0, (0, 1, 2))
    pl.semaphore_wait(credit, has_left.astype(jnp.int32) + has_right.astype(jnp.int32))

    share = 1.0 / rows

    def first_scalars():
        total = reduce_end(0)
        gamma, flat, square = total[0:1] * share, total[1:2] * share, total[2:3]
        alpha = gamma / (square + ridge * flat)
        scal[0:1] = wide(alpha)
        scal[1:2] = wide(ridge * alpha)
        scal[2:3] = wide(gamma)
        scal[3:4] = wide(flat)
        scal[4:5] = wide(square)

    def second_make(p):
        base = listed(p)
        terms = []
        for j in range(SIZE):
            e = (s_ref[index_ref[3, base + j]] * w_ref[...]).astype(BF16)
            terms.append(block_dot(x_all[p * SIZE + j], e).astype(BF16))
        store_terms(p, terms)

    def second_settle(p):
        base = listed(p)
        alpha, shift = scal[0:1], scal[1:2]
        made = []
        for j in range(SIZE):
            b = p * SIZE + j
            total = near_sum[b].astype(F32) + arrived[far, b].astype(F32)
            flat = d_ref[b].astype(F32)
            gradient = flat + low_ref[b].astype(F32) - alpha * total - shift * flat
            rounded = gradient.astype(BF16)
            low_ref[b] = rounded
            step = rounded.astype(F32)
            made.append(jnp.dot(x_all[b], rounded, preferred_element_type=F32))
            acc[3] += fold(gradient * gradient)
            acc[4] += fold(step * step)
            acc[5] += fold(step * flat)
        for j in range(SIZE):
            b = p * SIZE + j
            image = made[j] + image_ref[index_ref[2, base + j]]
            image_ref[b] = image
            final = ends_ref[base + j]
            weighted = w_ref[...] * image
            acc[6] += final * fold(weighted * image)
            acc[7] += final * fold(weighted * s_ref[b])

    last = FAR + LATE
    sweep(second_make, second_settle,
          [(LEAD - 1, lambda: reduce_middle(0)), (last, first_scalars)], last)

    reduce_start(1, (3, 4, 5, 6, 7))
    reduce_middle(1)
    total = reduce_end(1)
    alpha, gamma = scal[0:1], scal[2:3]
    flat, square = scal[3:4], scal[4:5]
    gamma_next = wide(total[0:1]) * share
    beta = gamma_next / gamma
    flat_next = wide(total[1:2]) * share + 2.0 * beta * wide(total[2:3]) * share + beta * beta * flat
    square_next = wide(total[3:4]) + 2.0 * beta * wide(total[4:5]) + beta * beta * square
    alpha_next = gamma_next / (square_next + ridge * flat_next)
    mixed = alpha + alpha_next * beta

    def mix(b, carry):
        image_ref[b] = mixed * s_ref[b] + alpha_next * image_ref[b]
        return carry

    lax.fori_loop(0, count, mix, 0, unroll=2)

    runs = coeffs_ref.shape[0] // run
    for u in range(runs):
        slot = xor(my_col, my_row * runs + u, bits)

        def own(i, carry):
            b = slot * run + i
            coeffs_ref[u * run + i] = mixed * d_ref[b].astype(F32) + alpha_next * low_ref[b].astype(F32)
            return carry

        lax.fori_loop(0, run, own, 0)


def fit(index, ends, x, targets, weight, run, ridge, shard):
    cols, rows = lax.axis_size("col"), lax.axis_size("row")
    count = run * cols
    samples = x.shape[0]
    pieces = count // SIZE
    block = (BLOCK, BLOCK)
    dma = pltpu.SemaphoreType.DMA
    return pl.pallas_call(
        functools.partial(fit_kernel, run, ridge),
        out_shape=(
            jax.ShapeDtypeStruct((count + 1, samples, BLOCK), F32),
            jax.ShapeDtypeStruct((shard,) + block, F32),
        ),
        in_specs=[SCALARS, SCALARS, WHOLE, WHOLE, WHOLE],
        out_specs=(WHOLE, WHOLE),
        scratch_shapes=[
            VMEM((count, samples, BLOCK), BF16), VMEM((count, samples, BLOCK), BF16),
            VMEM((count,) + block, BF16), VMEM((count,) + block, BF16),
            VMEM((2, count) + block, BF16),
            VMEM((count,) + block, BF16), VMEM((count,) + block, BF16),
            VMEM((count + 1, samples, BLOCK), F32),
            VMEM((8, 8, LANES), F32), VMEM((8, LANES), F32),
            VMEM((2, 8, LANES), F32), VMEM((2, cols, 8, LANES), F32),
            VMEM((2, 8, LANES), F32), VMEM((2, rows, 8, LANES), F32),
            dma((cols - 1,)), dma((cols - 1,)),
            dma((2, pieces)), dma((2, pieces)),
            dma((2, cols - 1)), dma((2, cols - 1)),
            dma((2, rows - 1)), dma((2, rows - 1)),
            pltpu.SemaphoreType.REGULAR,
        ],
        compiler_params=pltpu.CompilerParams(
            collective_id=2, has_side_effects=True, vmem_limit_bytes=66_000_000,
        ),
    )(index, ends, x, targets, weight)


def spread_kernel(index_ref, t_ref, image_ref, out_ref):
    def one(c, carry):
        place = pl.ds(pl.multiple_of(c * BLOCK, BLOCK), BLOCK)
        out_ref[:, place] = t_ref[:, place].astype(F32) - image_ref[index_ref[c]]
        return carry

    lax.fori_loop(0, index_ref.shape[0], one, 0, unroll=2)


def spread(index, targets, image):
    return pl.pallas_call(
        spread_kernel,
        out_shape=jax.ShapeDtypeStruct(targets.shape, F32),
        in_specs=[SCALARS, WHOLE, WHOLE],
        out_specs=WHOLE,
    )(index, targets, image)


def on_device(samples_x, targets, times, block_rows, block_cols):
    col_count = lax.axis_size("col")
    row_count = lax.axis_size("row")
    taxa_col = samples_x.shape[1]
    sample_count = samples_x.shape[0]
    column_count = taxa_col // BLOCK
    my_col = lax.axis_index("col")
    shard = block_rows.shape[0]
    count = shard * row_count
    run = count // col_count
    ridge = RIDGE_SHARE * sample_count * row_count
    weight = jnp.broadcast_to(
        (0.5 + times.astype(F32) / T_STEPS)[:, None], (sample_count, BLOCK)
    )
    places = jnp.pad(
        jnp.stack([block_rows, block_cols]), ((0, 6), (0, LANES - shard))
    )
    everywhere = gather_small(places, 1)
    rows_all = everywhere[:, :, 0, :shard].transpose(1, 0, 2).reshape(col_count, count)
    wanted = lax.dynamic_slice_in_dim(rows_all, my_col * run, run, 1) - my_col * column_count
    cols_mine = lax.dynamic_index_in_dim(everywhere[:, :, 1, :shard], my_col, 1, keepdims=False)
    cols = cols_mine.reshape(count) - my_col * column_count

    number = lax.iota(jnp.int32, count)
    slot = jnp.bitwise_xor(lax.div(number, run), my_col) * run + lax.rem(number, run)
    same = cols[:, None] == cols[None, :]
    final = jnp.max(jnp.where(same, slot[None, :], -1), axis=1)
    before = jnp.max(jnp.where(same & (slot[None, :] < slot[:, None]), slot[None, :], -1), axis=1)
    before = jnp.where(before < 0, count, before)
    held = lax.iota(jnp.int32, column_count)[:, None] == cols[None, :]
    end = jnp.max(jnp.where(held, slot[None, :], -1), axis=1)
    end = jnp.where(end < 0, count, end)
    index = jnp.stack([wanted.reshape(count), cols, before, final])

    image, coeffs = fit(index, (final == slot).astype(F32), samples_x, targets, weight, run, ridge, shard)
    return (coeffs, spread(end, targets, image))


def solution(mesh):
    placed = (P("row", "col"), P("row", "col"), P("row"), P(("col", "row")), P(("col", "row")))
    return jax.shard_map(
        on_device,
        mesh=mesh,
        in_specs=placed,
        out_specs=(P(("col", "row"), None, None), P("row", "col")),
        check_vma=False,
    )
```

```python
import functools

import jax
import jax.numpy as jnp
from jax import lax
from jax.experimental import pallas as pl
from jax.experimental.pallas import tpu as pltpu
from jax.sharding import PartitionSpec as P

BLOCK = 128
T_STEPS = 64
RIDGE_SHARE = 0.2
LANES = 128
SIZE = 3
LEAD = 4
FAR = 6
LATE = 1
STEPS = 4
VMEM = pltpu.VMEM
F32 = jnp.float32
BF16 = jnp.bfloat16
WHOLE = pl.BlockSpec(memory_space=pltpu.VMEM)
SCALARS = pl.BlockSpec(memory_space=pltpu.SMEM)
APART = pl.BlockSpec(memory_space=pl.ANY)
MESH = pl.DeviceIdType.MESH


def enter(axes):
    barrier = pltpu.get_barrier_semaphore()
    count = 0
    for axis in axes:
        n = lax.axis_size(axis)
        me = lax.axis_index(axis)
        for k in range(1, n):
            pl.semaphore_signal(
                barrier, inc=1, device_id={axis: lax.rem(me + k, n)}, device_id_type=MESH,
            )
        count += n - 1
    pl.semaphore_wait(barrier, count)


def push(src, dst, send, recv, axis, k):
    n = lax.axis_size(axis)
    return pltpu.make_async_remote_copy(
        src_ref=src, dst_ref=dst, send_sem=send, recv_sem=recv,
        device_id={axis: lax.rem(lax.axis_index(axis) + k, n)},
        device_id_type=MESH,
    )


def positions_kernel(taken, rows_ref, cols_ref, row_out, col_out, tile, by_col, by_row, send_a, recv_a, send_b, recv_b):
    cols, rows = lax.axis_size("col"), lax.axis_size("row")
    my_col, my_row = lax.axis_index("col"), lax.axis_index("row")
    ratio = cols // rows
    source = lax.div(my_col, ratio)
    alone = source == my_row
    barrier = pltpu.get_barrier_semaphore()

    def greet(col, row):
        pl.semaphore_signal(barrier, inc=1, device_id={"col": col, "row": row}, device_id_type=MESH)

    greet_self = jnp.where(alone, 1, 0)
    for k in range(1, cols):
        greet(lax.rem(my_col + k, cols), source)
    pl.when(source != my_row)(lambda: greet(my_col, source))
    for k in range(1, rows):
        greet(my_col, lax.rem(my_row + k, rows))
    shard = rows_ref.shape[1]
    tile[...] = jnp.zeros_like(tile)
    tile[0:1, 0:shard] = rows_ref[...]
    tile[1:2, 0:shard] = cols_ref[...]
    pl.semaphore_wait(barrier, ratio * rows - greet_self + rows - 1)

    def to_reader(j, row, k):
        return pltpu.make_async_remote_copy(
            src_ref=tile, dst_ref=by_col.at[my_col], send_sem=send_a.at[k], recv_sem=recv_a.at[my_col],
            device_id={"col": my_row * ratio + j, "row": row}, device_id_type=MESH,
        )

    def to_group(k):
        return pltpu.make_async_remote_copy(
            src_ref=tile, dst_ref=by_row.at[my_row], send_sem=send_b.at[k], recv_sem=recv_b.at[my_row],
            device_id={"row": lax.rem(my_row + k, rows)}, device_id_type=MESH,
        )

    def each(act):
        for j in range(ratio):
            for row in range(rows):
                other = (my_row * ratio + j != my_col) | (my_row != row)
                pl.when(other)(lambda j=j, row=row: act(to_reader(j, row, j * rows + row)))

    each(lambda copy: copy.start())
    for k in range(1, rows):
        to_group(k).start()
    by_row[my_row] = tile[...]

    @pl.when(alone)
    def _():
        by_col[my_col] = tile[...]

    def from_col(col):
        return pltpu.make_async_remote_copy(
            src_ref=tile, dst_ref=by_col.at[col], send_sem=send_a.at[0], recv_sem=recv_a.at[col],
            device_id={"col": col, "row": source}, device_id_type=MESH,
        )

    def from_row(row):
        return pltpu.make_async_remote_copy(
            src_ref=tile, dst_ref=by_row.at[row], send_sem=send_b.at[0], recv_sem=recv_b.at[row],
            device_id={"row": row}, device_id_type=MESH,
        )

    for k in range(1, cols):
        from_col(lax.rem(my_col + k, cols)).wait_recv()
    pl.when(source != my_row)(lambda: from_col(my_col).wait_recv())
    for k in range(1, rows):
        from_row(lax.rem(my_row + k, rows)).wait_recv()
    for col in range(cols):
        row_out[col:col + 1, :] = by_col[col, 0:1, :] - my_col * taken
    for row in range(rows):
        col_out[row:row + 1, :] = by_row[row, 1:2, :] - my_col * taken
    each(lambda copy: copy.wait_send())
    for k in range(1, rows):
        to_group(k).wait_send()


def positions(block_rows, block_cols, taken, call_id):
    cols, rows = lax.axis_size("col"), lax.axis_size("row")
    dma = pltpu.SemaphoreType.DMA
    return pl.pallas_call(
        functools.partial(positions_kernel, taken),
        out_shape=(
            jax.ShapeDtypeStruct((cols, LANES), jnp.int32), jax.ShapeDtypeStruct((rows, LANES), jnp.int32),
        ),
        in_specs=[WHOLE, WHOLE],
        out_specs=(WHOLE, WHOLE),
        scratch_shapes=[
            VMEM((8, LANES), jnp.int32), VMEM((cols, 8, LANES), jnp.int32), VMEM((rows, 8, LANES), jnp.int32),
            dma((cols,)), dma((cols,)), dma((rows,)), dma((rows,)),
        ],
        compiler_params=pltpu.CompilerParams(collective_id=call_id, has_side_effects=True),
    )(block_rows[None], block_cols[None])


def block_dot(x, e):
    return lax.dot_general(x, e, (((0,), (0,)), ((), ())), preferred_element_type=F32)


def fold(values):
    return jnp.sum(values.reshape(values.shape[0] // 8, 8, BLOCK), axis=0)


def xor(a, b, bits):
    out = 0
    for i in range(bits):
        x = lax.rem(lax.div(a, 2 ** i), 2)
        if isinstance(b, int):
            y = (b >> i) & 1
        else:
            y = lax.rem(lax.div(b, 2 ** i), 2)
        out = out + (x + y - 2 * x * y) * 2 ** i
    return out


def fit_kernel(
    run, ridge, row_ref, col_ref, index_ref, ends_ref, times_ref, x_hbm, t_hbm, image_hbm, coeffs_ref,
    x_ref, t_ref, w_ref, image_ref, give, x_all, near_sum, far_sum, arrived, d_ref, low_ref, s_ref, acc, scal, mine, by_col, line, by_row,
    send_x, recv_x, send_z, recv_z, send_c, recv_c, send_r, recv_r, credit, load, leave,
):
    cols, rows = lax.axis_size("col"), lax.axis_size("row")
    my_col, my_row = lax.axis_index("col"), lax.axis_index("row")
    bits = (cols - 1).bit_length()
    count = x_all.shape[0]
    pieces = count // SIZE
    per_run = run // SIZE
    shard = coeffs_ref.shape[0]
    load_x = pltpu.make_async_copy(x_hbm, x_ref, load.at[0])
    load_t = pltpu.make_async_copy(t_hbm, t_ref, load.at[1])
    load_x.start()
    load_t.start()
    weight = 0.5 + times_ref[...].astype(F32) / T_STEPS
    w_ref[...] = jnp.transpose(jnp.broadcast_to(weight, (BLOCK, weight.shape[1])))
    acc[...] = jnp.zeros_like(acc)
    s_ref[count] = jnp.zeros((BLOCK, BLOCK), F32)
    image_ref[count] = jnp.zeros((BLOCK, BLOCK), F32)
    enter(("col", "row"))
    load_x.wait()

    def select(s, target):
        group = xor(my_col, s, bits)
        base = lax.rem(my_col, shard // run) * run

        def one(i, carry):
            column = row_ref[group, base + i] * BLOCK
            target[s * run + i] = x_ref[:, pl.ds(column, BLOCK)]
            return carry

        lax.fori_loop(0, run, one, 0, unroll=3)

    def exchange(s):
        place = pl.ds(s * run, run)
        return pltpu.make_async_remote_copy(
            src_ref=give.at[place], dst_ref=x_all.at[place],
            send_sem=send_x.at[s - 1], recv_sem=recv_x.at[s - 1],
            device_id={"col": xor(my_col, s, bits)}, device_id_type=MESH,
        )

    def offer(s):
        select(s, give)
        exchange(s).start()

    select(0, x_all)
    for s in range(1, min(4, cols)):
        offer(s)
    later = [(s - 4, functools.partial(offer, s)) for s in range(4, cols)]
    load_t.wait()

    near = lax.div(2 * my_row, rows)
    far = 1 - near
    has_near = jnp.logical_and(my_row > 0, my_row < rows - 1)
    at_end = (my_row == 0) | (my_row == rows - 1)
    to_far = my_row + 1 - 2 * near
    to_near = my_row - 1 + 2 * near

    def forth(p):
        place = pl.ds(p * SIZE, SIZE)
        return pltpu.make_async_remote_copy(
            src_ref=near_sum.at[place], dst_ref=arrived.at[near, place],
            send_sem=send_z.at[near, p], recv_sem=recv_z.at[near, p],
            device_id={"row": to_far}, device_id_type=MESH,
        )

    def back(p):
        place = pl.ds(p * SIZE, SIZE)
        return pltpu.make_async_remote_copy(
            src_ref=far_sum.at[place], dst_ref=arrived.at[far, place],
            send_sem=send_z.at[far, p], recv_sem=recv_z.at[far, p],
            device_id={"row": to_near}, device_id_type=MESH,
        )

    def listed(p):
        s = lax.div(p, per_run)
        return xor(my_col, s, bits) * run + (p - s * per_run) * SIZE

    def store_terms(p, terms):
        for j in range(SIZE):
            near_sum[p * SIZE + j] = terms[j]
            far_sum[p * SIZE + j] = terms[j]
        pl.when(at_end)(lambda: forth(p).start())

    def pass_forth(p):
        forth(p).wait_recv()
        for j in range(SIZE):
            b = p * SIZE + j
            near_sum[b] = (far_sum[b].astype(F32) + arrived[near, b].astype(F32)).astype(BF16)
        forth(p).start()

    def pass_back(p):
        back(p).wait_recv()

        @pl.when(has_near)
        def _():
            for j in range(SIZE):
                b = p * SIZE + j
                far_sum[b] = (far_sum[b].astype(F32) + arrived[far, b].astype(F32)).astype(BF16)
            back(p).start()

    def sweep(make, settle, hooks, last):
        def body(q, carry):
            pl.when(q < pieces)(lambda: make(q))
            pl.when(has_near & (q >= LEAD) & (q < pieces + LEAD))(lambda: pass_forth(q - LEAD))
            pl.when((q >= FAR) & (q < pieces + FAR))(lambda: pass_back(q - FAR))
            for when, hook in hooks:
                pl.when(q == when)(hook)
            pl.when(q >= last)(lambda: settle(q - last))
            return carry

        lax.fori_loop(0, pieces + last, body, 0)

        def drain(p, carry):
            forth(p).wait_send()
            pl.when(has_near)(lambda: back(p).wait_send())
            return carry

        lax.fori_loop(0, pieces, drain, 0)

    def over_col(a, k):
        return push(mine.at[a], by_col.at[a, my_col], send_c.at[a, k - 1], recv_c.at[a, k - 1], "col", k)

    def over_row(a, k):
        return push(line.at[a], by_row.at[a, my_row], send_r.at[a, k - 1], recv_r.at[a, k - 1], "row", k)

    def reduce_start(a, wanted):
        tile = jnp.concatenate(
            [jnp.sum(acc[j], axis=0, keepdims=True) for j in wanted]
            + [jnp.zeros((8 - len(wanted), LANES), F32)], axis=0,
        )
        mine[a] = tile
        by_col[a, my_col] = tile
        for k in range(1, cols):
            over_col(a, k).start()

    def reduce_middle(a):
        for k in range(1, cols):
            over_col(a, k).wait()
        tile = by_col[a, 0]
        for j in range(1, cols):
            tile = tile + by_col[a, j]
        line[a] = tile
        by_row[a, my_row] = tile
        for k in range(1, rows):
            over_row(a, k).start()

    def reduce_end(a):
        for k in range(1, rows):
            over_row(a, k).wait()
        tile = by_row[a, 0]
        for j in range(1, rows):
            tile = tile + by_row[a, j]
        return jnp.sum(tile, axis=1, keepdims=True)

    def wide(value):
        return jnp.broadcast_to(value, (1, LANES))

    def first_make(p):
        s = lax.div(p, per_run)

        @pl.when((s > 0) & (s * per_run == p))
        def _():
            place = pl.ds(s * run, run)
            pltpu.make_async_remote_copy(
                src_ref=give.at[place], dst_ref=x_all.at[place],
                send_sem=send_x.at[s - 1], recv_sem=recv_x.at[s - 1],
                device_id={"col": xor(my_col, s, bits)}, device_id_type=MESH,
            ).wait_recv()

        base = listed(p)
        terms = []
        for j in range(SIZE):
            column = col_ref[lax.div(base + j, shard), lax.rem(base + j, shard)]
            place = pl.ds(column * BLOCK, BLOCK)
            e = (t_ref[:, place].astype(F32) * w_ref[...]).astype(BF16)
            terms.append(block_dot(x_all[p * SIZE + j], e).astype(BF16))
        store_terms(p, terms)

    def first_settle(p):
        base = listed(p)
        made = []
        for j in range(SIZE):
            b = p * SIZE + j
            total = near_sum[b].astype(F32) + arrived[far, b].astype(F32)
            rounded = total.astype(BF16)
            flat = rounded.astype(F32)
            d_ref[b] = rounded
            low_ref[b] = (total - flat).astype(BF16)
            made.append(jnp.dot(x_all[b], rounded, preferred_element_type=F32))
            acc[0] += fold(total * total)
            acc[1] += fold(flat * flat)
        for j in range(SIZE):
            b = p * SIZE + j
            image = made[j] + s_ref[index_ref[0, base + j]]
            s_ref[b] = image
            acc[2] += ends_ref[base + j] * fold(w_ref[...] * image * image)

    sweep(first_make, first_settle, later, FAR)
    for s in range(1, cols):
        exchange(s).wait_send()

    def greet(other):
        pl.semaphore_signal(credit, inc=1, device_id={"row": other}, device_id_type=MESH)

    has_left, has_right = my_row > 0, my_row < rows - 1
    pl.when(has_left)(lambda: greet(my_row - 1))
    pl.when(has_right)(lambda: greet(my_row + 1))
    reduce_start(0, (0, 1, 2))
    pl.semaphore_wait(credit, has_left.astype(jnp.int32) + has_right.astype(jnp.int32))

    share = 1.0 / rows

    def first_scalars():
        total = reduce_end(0)
        gamma, flat, square = total[0:1] * share, total[1:2] * share, total[2:3]
        alpha = gamma / (square + ridge * flat)
        scal[0:1] = wide(alpha)
        scal[1:2] = wide(ridge * alpha)
        scal[2:3] = wide(gamma)
        scal[3:4] = wide(flat)
        scal[4:5] = wide(square)

    def second_make(p):
        base = listed(p)
        terms = []
        for j in range(SIZE):
            e = (s_ref[index_ref[1, base + j]] * w_ref[...]).astype(BF16)
            terms.append(block_dot(x_all[p * SIZE + j], e).astype(BF16))
        store_terms(p, terms)

    def second_settle(p):
        base = listed(p)
        alpha, shift = scal[0:1], scal[1:2]
        made = []
        for j in range(SIZE):
            b = p * SIZE + j
            total = near_sum[b].astype(F32) + arrived[far, b].astype(F32)
            flat = d_ref[b].astype(F32)
            gradient = flat + low_ref[b].astype(F32) - alpha * total - shift * flat
            rounded = gradient.astype(BF16)
            low_ref[b] = rounded
            step = rounded.astype(F32)
            made.append(jnp.dot(x_all[b], rounded, preferred_element_type=F32))
            acc[3] += fold(gradient * gradient)
            acc[4] += fold(step * step)
            acc[5] += fold(step * flat)
        for j in range(SIZE):
            b = p * SIZE + j
            image = made[j] + image_ref[index_ref[0, base + j]]
            image_ref[b] = image
            final = ends_ref[base + j]
            weighted = w_ref[...] * image
            acc[6] += final * fold(weighted * image)
            acc[7] += final * fold(weighted * s_ref[b])

    last = FAR + LATE
    sweep(second_make, second_settle,
          [(LEAD - 1, lambda: reduce_middle(0)), (last, first_scalars)], last)

    reduce_start(1, (3, 4, 5, 6, 7))
    reduce_middle(1)
    total = reduce_end(1)
    alpha, gamma = scal[0:1], scal[2:3]
    flat, square = scal[3:4], scal[4:5]
    gamma_next = wide(total[0:1]) * share
    beta = gamma_next / gamma
    flat_next = wide(total[1:2]) * share + 2.0 * beta * wide(total[2:3]) * share + beta * beta * flat
    square_next = wide(total[3:4]) + 2.0 * beta * wide(total[4:5]) + beta * beta * square
    alpha_next = gamma_next / (square_next + ridge * flat_next)
    mixed = alpha + alpha_next * beta

    def leaving(s):
        place = pl.ds(s * run, run)
        return pltpu.make_async_copy(give.at[place], image_hbm.at[place], leave.at[s])

    for s in range(cols):
        def mix(i, carry):
            b = s * run + i
            give[b] = (mixed * s_ref[b] + alpha_next * image_ref[b]).astype(BF16)
            return carry

        lax.fori_loop(0, run, mix, 0, unroll=3)
        leaving(s).start()

    runs = coeffs_ref.shape[0] // run
    for u in range(runs):
        slot = xor(my_col, my_row * runs + u, bits)

        def own(i, carry):
            b = slot * run + i
            coeffs_ref[u * run + i] = mixed * d_ref[b].astype(F32) + alpha_next * low_ref[b].astype(F32)
            return carry

        lax.fori_loop(0, run, own, 0)
    for s in range(cols):
        leaving(s).wait()


def fit(row_places, col_places, index, ends, times, x, targets, run, ridge, shard):
    cols, rows = lax.axis_size("col"), lax.axis_size("row")
    count = run * cols
    samples = x.shape[0]
    pieces = count // SIZE
    block = (BLOCK, BLOCK)
    dma = pltpu.SemaphoreType.DMA
    return pl.pallas_call(
        functools.partial(fit_kernel, run, ridge),
        out_shape=(
            jax.ShapeDtypeStruct((count, samples, BLOCK), BF16),
            jax.ShapeDtypeStruct((shard,) + block, F32),
        ),
        in_specs=[SCALARS, SCALARS, SCALARS, SCALARS, WHOLE, APART, APART],
        out_specs=(APART, WHOLE),
        scratch_shapes=[
            VMEM(x.shape, BF16), VMEM(x.shape, BF16), VMEM((samples, BLOCK), F32),
            VMEM((count + 1, samples, BLOCK), F32),
            VMEM((count, samples, BLOCK), BF16), VMEM((count, samples, BLOCK), BF16),
            VMEM((count,) + block, BF16), VMEM((count,) + block, BF16),
            VMEM((2, count) + block, BF16),
            VMEM((count,) + block, BF16), VMEM((count,) + block, BF16),
            VMEM((count + 1, samples, BLOCK), F32),
            VMEM((8, 8, LANES), F32), VMEM((8, LANES), F32),
            VMEM((2, 8, LANES), F32), VMEM((2, cols, 8, LANES), F32),
            VMEM((2, 8, LANES), F32), VMEM((2, rows, 8, LANES), F32),
            dma((cols - 1,)), dma((cols - 1,)),
            dma((2, pieces)), dma((2, pieces)),
            dma((2, cols - 1)), dma((2, cols - 1)),
            dma((2, rows - 1)), dma((2, rows - 1)),
            pltpu.SemaphoreType.REGULAR, dma((2,)), dma((cols,)),
        ],
        compiler_params=pltpu.CompilerParams(
            collective_id=2, has_side_effects=True, vmem_limit_bytes=66_000_000,
        ),
    )(row_places, col_places, index, ends, times, x, targets)


def spread_kernel(index_ref, t_ref, image_ref, out_ref):
    wide = t_ref.shape[1] // BLOCK
    first = pl.program_id(0) * wide
    count = image_ref.shape[0]

    def one(c, carry):
        place = pl.ds(pl.multiple_of(c * BLOCK, BLOCK), BLOCK)
        held = index_ref[first + c]
        keep = jnp.where(held < count, 1.0, 0.0)
        out_ref[:, place] = t_ref[:, place].astype(F32) - keep * image_ref[jnp.minimum(held, count - 1)].astype(F32)
        return carry

    lax.fori_loop(0, wide, one, 0, unroll=2)


def spread(index, targets, image):
    samples, taxa = targets.shape
    wide = taxa // STEPS
    return pl.pallas_call(
        spread_kernel,
        grid=(STEPS,),
        out_shape=jax.ShapeDtypeStruct(targets.shape, F32),
        in_specs=[SCALARS, pl.BlockSpec((samples, wide), lambda i: (0, i)), WHOLE],
        out_specs=pl.BlockSpec((samples, wide), lambda i: (0, i)),
    )(index, targets, image)


def on_device(samples_x, targets, times, block_rows, block_cols):
    col_count = lax.axis_size("col")
    row_count = lax.axis_size("row")
    taxa_col = samples_x.shape[1]
    sample_count = samples_x.shape[0]
    column_count = taxa_col // BLOCK
    my_col = lax.axis_index("col")
    shard = block_rows.shape[0]
    count = shard * row_count
    run = count // col_count
    ridge = RIDGE_SHARE * sample_count * row_count
    row_places, col_places = positions(block_rows, block_cols, column_count, 1)
    cols = col_places[:, :shard].reshape(count)

    number = lax.iota(jnp.int32, count)
    slot = jnp.bitwise_xor(lax.div(number, run), my_col) * run + lax.rem(number, run)
    same = cols[:, None] == cols[None, :]
    final = jnp.max(jnp.where(same, slot[None, :], -1), axis=1)
    before = jnp.max(jnp.where(same & (slot[None, :] < slot[:, None]), slot[None, :], -1), axis=1)
    before = jnp.where(before < 0, count, before)
    held = lax.iota(jnp.int32, column_count)[:, None] == cols[None, :]
    end = jnp.max(jnp.where(held, slot[None, :], -1), axis=1)
    end = jnp.where(end < 0, count, end)
    index = jnp.stack([before, final])

    ends = (final == slot).astype(F32)
    image, coeffs = fit(row_places, col_places, index, ends, times[None], samples_x, targets, run, ridge, shard)
    return (coeffs, spread(end, targets, image))


def solution(mesh):
    placed = (P("row", "col"), P("row", "col"), P("row"), P(("col", "row")), P(("col", "row")))
    return jax.shard_map(
        on_device,
        mesh=mesh,
        in_specs=placed,
        out_specs=(P(("col", "row"), None, None), P("row", "col")),
        check_vma=False,
    )
```

```python
import functools

import jax
import jax.numpy as jnp
from jax import lax
from jax.experimental import pallas as pl
from jax.experimental.pallas import tpu as pltpu
from jax.sharding import PartitionSpec as P

BLOCK = 128
T_STEPS = 64
RIDGE_SHARE = 0.2
LANES = 128
SIZE = 1
LEAD = 6
FAR = 11
EDGE = 24
LATE = 2
PARTS = 6
VMEM = pltpu.VMEM
F32 = jnp.float32
BF16 = jnp.bfloat16
WHOLE = pl.BlockSpec(memory_space=pltpu.VMEM)
SCALARS = pl.BlockSpec(memory_space=pltpu.SMEM)
APART = pl.BlockSpec(memory_space=pl.ANY)
MESH = pl.DeviceIdType.MESH


def enter(axes):
    barrier = pltpu.get_barrier_semaphore()
    count = 0
    for axis in axes:
        n = lax.axis_size(axis)
        me = lax.axis_index(axis)
        for k in range(1, n):
            pl.semaphore_signal(
                barrier, inc=1, device_id={axis: lax.rem(me + k, n)}, device_id_type=MESH,
            )
        count += n - 1
    pl.semaphore_wait(barrier, count)


def push(src, dst, send, recv, axis, k):
    n = lax.axis_size(axis)
    return pltpu.make_async_remote_copy(
        src_ref=src, dst_ref=dst, send_sem=send, recv_sem=recv,
        device_id={axis: lax.rem(lax.axis_index(axis) + k, n)},
        device_id_type=MESH,
    )


def positions_kernel(taken, rows_ref, cols_ref, row_out, col_out, tile, by_col, by_row, send_a, recv_a, send_b, recv_b):
    cols, rows = lax.axis_size("col"), lax.axis_size("row")
    my_col, my_row = lax.axis_index("col"), lax.axis_index("row")
    ratio = cols // rows
    source = lax.div(my_col, ratio)
    alone = source == my_row
    barrier = pltpu.get_barrier_semaphore()

    def greet(col, row):
        pl.semaphore_signal(barrier, inc=1, device_id={"col": col, "row": row}, device_id_type=MESH)

    greet_self = jnp.where(alone, 1, 0)
    for k in range(1, cols):
        greet(lax.rem(my_col + k, cols), source)
    pl.when(source != my_row)(lambda: greet(my_col, source))
    for k in range(1, rows):
        greet(my_col, lax.rem(my_row + k, rows))
    shard = rows_ref.shape[1]
    tile[...] = jnp.zeros_like(tile)
    tile[0:1, 0:shard] = rows_ref[...]
    tile[1:2, 0:shard] = cols_ref[...]
    pl.semaphore_wait(barrier, ratio * rows - greet_self + rows - 1)

    def to_reader(j, row, k):
        return pltpu.make_async_remote_copy(
            src_ref=tile, dst_ref=by_col.at[my_col], send_sem=send_a.at[k], recv_sem=recv_a.at[my_col],
            device_id={"col": my_row * ratio + j, "row": row}, device_id_type=MESH,
        )

    def to_group(k):
        return pltpu.make_async_remote_copy(
            src_ref=tile, dst_ref=by_row.at[my_row], send_sem=send_b.at[k], recv_sem=recv_b.at[my_row],
            device_id={"row": lax.rem(my_row + k, rows)}, device_id_type=MESH,
        )

    def each(act):
        for j in range(ratio):
            for row in range(rows):
                other = (my_row * ratio + j != my_col) | (my_row != row)
                pl.when(other)(lambda j=j, row=row: act(to_reader(j, row, j * rows + row)))

    each(lambda copy: copy.start())
    for k in range(1, rows):
        to_group(k).start()
    by_row[my_row] = tile[...]

    @pl.when(alone)
    def _():
        by_col[my_col] = tile[...]

    def from_col(col):
        return pltpu.make_async_remote_copy(
            src_ref=tile, dst_ref=by_col.at[col], send_sem=send_a.at[0], recv_sem=recv_a.at[col],
            device_id={"col": col, "row": source}, device_id_type=MESH,
        )

    def from_row(row):
        return pltpu.make_async_remote_copy(
            src_ref=tile, dst_ref=by_row.at[row], send_sem=send_b.at[0], recv_sem=recv_b.at[row],
            device_id={"row": row}, device_id_type=MESH,
        )

    for k in range(1, cols):
        from_col(lax.rem(my_col + k, cols)).wait_recv()
    pl.when(source != my_row)(lambda: from_col(my_col).wait_recv())
    for k in range(1, rows):
        from_row(lax.rem(my_row + k, rows)).wait_recv()
    for col in range(cols):
        row_out[col:col + 1, :] = by_col[col, 0:1, :] - my_col * taken
    for row in range(rows):
        col_out[row:row + 1, :] = by_row[row, 1:2, :] - my_col * taken
    each(lambda copy: copy.wait_send())
    for k in range(1, rows):
        to_group(k).wait_send()


def positions(block_rows, block_cols, taken, call_id):
    cols, rows = lax.axis_size("col"), lax.axis_size("row")
    dma = pltpu.SemaphoreType.DMA
    return pl.pallas_call(
        functools.partial(positions_kernel, taken),
        out_shape=(
            jax.ShapeDtypeStruct((cols, LANES), jnp.int32), jax.ShapeDtypeStruct((rows, LANES), jnp.int32),
        ),
        in_specs=[WHOLE, WHOLE],
        out_specs=(WHOLE, WHOLE),
        scratch_shapes=[
            VMEM((8, LANES), jnp.int32), VMEM((cols, 8, LANES), jnp.int32), VMEM((rows, 8, LANES), jnp.int32),
            dma((cols,)), dma((cols,)), dma((rows,)), dma((rows,)),
        ],
        compiler_params=pltpu.CompilerParams(collective_id=call_id, has_side_effects=True),
    )(block_rows[None], block_cols[None])


def block_dot(x, e):
    return lax.dot_general(x, e, (((0,), (0,)), ((), ())), preferred_element_type=F32)


def fold(values):
    return jnp.sum(values.reshape(values.shape[0] // 8, 8, BLOCK), axis=0)


def xor(a, b, bits):
    out = 0
    for i in range(bits):
        x = lax.rem(lax.div(a, 2 ** i), 2)
        if isinstance(b, int):
            y = (b >> i) & 1
        else:
            y = lax.rem(lax.div(b, 2 ** i), 2)
        out = out + (x + y - 2 * x * y) * 2 ** i
    return out


def fit_kernel(
    run, ridge, row_ref, col_ref, index_ref, ends_ref, last_ref, times_ref, x_hbm, t_hbm, residual_hbm, coeffs_ref,
    x_ref, t_ref, w_ref, image_ref, give, x_all, near_sum, far_sum, arrived, d_ref, low_ref, s_ref, acc, scal, mine, by_col, line, by_row,
    send_x, recv_x, send_z, recv_z, send_c, recv_c, send_r, recv_r, credit, load, leave,
):
    cols, rows = lax.axis_size("col"), lax.axis_size("row")
    my_col, my_row = lax.axis_index("col"), lax.axis_index("row")
    bits = (cols - 1).bit_length()
    count = x_all.shape[0]
    pieces = count // SIZE
    per_run = run // SIZE
    shard = coeffs_ref.shape[0]
    load_x = pltpu.make_async_copy(x_hbm, x_ref, load.at[0])
    load_t = pltpu.make_async_copy(t_hbm, t_ref, load.at[1])
    load_x.start()
    load_t.start()
    weight = 0.5 + times_ref[...].astype(F32) / T_STEPS
    w_ref[...] = jnp.transpose(jnp.broadcast_to(weight, (BLOCK, weight.shape[1])))
    acc[...] = jnp.zeros_like(acc)
    s_ref[count] = jnp.zeros((BLOCK, BLOCK), F32)
    image_ref[count] = jnp.zeros((BLOCK, BLOCK), F32)
    enter(("col", "row"))
    load_x.wait()

    def select(s, target):
        group = xor(my_col, s, bits)
        base = lax.rem(my_col, shard // run) * run

        def one(i, carry):
            column = row_ref[group, base + i] * BLOCK
            target[s * run + i] = x_ref[:, pl.ds(column, BLOCK)]
            return carry

        lax.fori_loop(0, run, one, 0, unroll=3)

    def exchange(s):
        place = pl.ds(s * run, run)
        return pltpu.make_async_remote_copy(
            src_ref=give.at[place], dst_ref=x_all.at[place],
            send_sem=send_x.at[s - 1], recv_sem=recv_x.at[s - 1],
            device_id={"col": xor(my_col, s, bits)}, device_id_type=MESH,
        )

    def offer(s):
        select(s, give)
        exchange(s).start()

    select(0, x_all)
    for s in range(1, min(4, cols)):
        offer(s)
    later = [(s - 4, functools.partial(offer, s)) for s in range(4, cols)]
    load_t.wait()

    near = lax.div(2 * my_row, rows)
    far = 1 - near
    has_near = jnp.logical_and(my_row > 0, my_row < rows - 1)
    at_end = (my_row == 0) | (my_row == rows - 1)
    to_far = my_row + 1 - 2 * near
    to_near = my_row - 1 + 2 * near

    def forth(p):
        place = pl.ds(p * SIZE, SIZE)
        return pltpu.make_async_remote_copy(
            src_ref=near_sum.at[place], dst_ref=arrived.at[near, place],
            send_sem=send_z.at[near, p], recv_sem=recv_z.at[near, p],
            device_id={"row": to_far}, device_id_type=MESH,
        )

    def back(p):
        place = pl.ds(p * SIZE, SIZE)
        return pltpu.make_async_remote_copy(
            src_ref=far_sum.at[place], dst_ref=arrived.at[far, place],
            send_sem=send_z.at[far, p], recv_sem=recv_z.at[far, p],
            device_id={"row": to_near}, device_id_type=MESH,
        )

    def listed(p):
        s = lax.div(p, per_run)
        return xor(my_col, s, bits) * run + (p - s * per_run) * SIZE

    def store_terms(p, terms):
        for j in range(SIZE):
            near_sum[p * SIZE + j] = terms[j]
            far_sum[p * SIZE + j] = terms[j]
        pl.when(at_end)(lambda: forth(p).start())

    def pass_forth(p):
        forth(p).wait_recv()
        for j in range(SIZE):
            b = p * SIZE + j
            near_sum[b] = (far_sum[b].astype(F32) + arrived[near, b].astype(F32)).astype(BF16)
        forth(p).start()

    def pass_back(p):
        back(p).wait_recv()

        @pl.when(has_near)
        def _():
            for j in range(SIZE):
                b = p * SIZE + j
                far_sum[b] = (far_sum[b].astype(F32) + arrived[far, b].astype(F32)).astype(BF16)
            back(p).start()

    lag = jnp.where(at_end, EDGE, FAR)

    def sweep(make, settle, hooks, late):
        def body(q, carry):
            pl.when(q < pieces)(lambda: make(q))
            pl.when(has_near & (q >= LEAD) & (q < pieces + LEAD))(lambda: pass_forth(q - LEAD))
            pl.when((q >= lag) & (q < pieces + lag))(lambda: pass_back(q - lag))
            for when, hook in hooks:
                pl.when(q == when)(hook)
            pl.when((q >= lag + late) & (q < pieces + lag + late))(lambda: settle(q - lag - late))
            return carry

        lax.fori_loop(0, pieces + EDGE + late, body, 0)

    def over_col(a, k):
        return push(mine.at[a], by_col.at[a, my_col], send_c.at[a, k - 1], recv_c.at[a, k - 1], "col", k)

    def over_row(a, k):
        return push(line.at[a], by_row.at[a, my_row], send_r.at[a, k - 1], recv_r.at[a, k - 1], "row", k)

    def reduce_start(a, wanted):
        tile = jnp.concatenate(
            [jnp.sum(acc[j], axis=0, keepdims=True) for j in wanted]
            + [jnp.zeros((8 - len(wanted), LANES), F32)], axis=0,
        )
        mine[a] = tile
        by_col[a, my_col] = tile
        for k in range(1, cols):
            over_col(a, k).start()

    def reduce_middle(a):
        for k in range(1, cols):
            over_col(a, k).wait()
        tile = by_col[a, 0]
        for j in range(1, cols):
            tile = tile + by_col[a, j]
        line[a] = tile
        by_row[a, my_row] = tile
        for k in range(1, rows):
            over_row(a, k).start()

    def reduce_end(a):
        for k in range(1, rows):
            over_row(a, k).wait()
        tile = by_row[a, 0]
        for j in range(1, rows):
            tile = tile + by_row[a, j]
        return jnp.sum(tile, axis=1, keepdims=True)

    def wide(value):
        return jnp.broadcast_to(value, (1, LANES))

    def first_make(p):
        s = lax.div(p, per_run)

        @pl.when((s > 0) & (s * per_run == p))
        def _():
            place = pl.ds(s * run, run)
            pltpu.make_async_remote_copy(
                src_ref=give.at[place], dst_ref=x_all.at[place],
                send_sem=send_x.at[s - 1], recv_sem=recv_x.at[s - 1],
                device_id={"col": xor(my_col, s, bits)}, device_id_type=MESH,
            ).wait_recv()

        base = listed(p)
        terms = []
        for j in range(SIZE):
            column = col_ref[lax.div(base + j, shard), lax.rem(base + j, shard)]
            place = pl.ds(column * BLOCK, BLOCK)
            e = (t_ref[:, place].astype(F32) * w_ref[...]).astype(BF16)
            terms.append(block_dot(x_all[p * SIZE + j], e).astype(BF16))
        store_terms(p, terms)

    def first_settle(p):
        forth(p).wait_send()
        base = listed(p)
        made = []
        for j in range(SIZE):
            b = p * SIZE + j
            total = near_sum[b].astype(F32) + arrived[far, b].astype(F32)
            rounded = total.astype(BF16)
            flat = rounded.astype(F32)
            d_ref[b] = rounded
            low_ref[b] = (total - flat).astype(BF16)
            made.append(jnp.dot(x_all[b], rounded, preferred_element_type=F32))
            acc[0] += fold(total * total)
            acc[1] += fold(flat * flat)
        for j in range(SIZE):
            b = p * SIZE + j
            image = made[j] + s_ref[index_ref[0, base + j]]
            s_ref[b] = image
            acc[2] += ends_ref[base + j] * fold(w_ref[...] * image * image)

    sweep(first_make, first_settle, later, 0)
    def greet(other):
        pl.semaphore_signal(credit, inc=1, device_id={"row": other}, device_id_type=MESH)

    has_left, has_right = my_row > 0, my_row < rows - 1
    pl.when(has_left)(lambda: greet(my_row - 1))
    pl.when(has_right)(lambda: greet(my_row + 1))
    reduce_start(0, (0, 1, 2))
    pl.semaphore_wait(credit, has_left.astype(jnp.int32) + has_right.astype(jnp.int32))

    share = 1.0 / rows

    def first_scalars():
        total = reduce_end(0)
        gamma, flat, square = total[0:1] * share, total[1:2] * share, total[2:3]
        alpha = gamma / (square + ridge * flat)
        scal[0:1] = wide(alpha)
        scal[1:2] = wide(ridge * alpha)
        scal[2:3] = wide(gamma)
        scal[3:4] = wide(flat)
        scal[4:5] = wide(square)

    def second_make(p):
        pl.when(has_near)(lambda: back(p).wait_send())
        base = listed(p)
        terms = []
        for j in range(SIZE):
            e = (s_ref[index_ref[1, base + j]] * w_ref[...]).astype(BF16)
            terms.append(block_dot(x_all[p * SIZE + j], e).astype(BF16))
        store_terms(p, terms)

    def second_settle(p):
        forth(p).wait_send()
        base = listed(p)
        alpha, shift = scal[0:1], scal[1:2]
        made = []
        for j in range(SIZE):
            b = p * SIZE + j
            total = near_sum[b].astype(F32) + arrived[far, b].astype(F32)
            flat = d_ref[b].astype(F32)
            gradient = flat + low_ref[b].astype(F32) - alpha * total - shift * flat
            rounded = gradient.astype(BF16)
            low_ref[b] = rounded
            step = rounded.astype(F32)
            made.append(jnp.dot(x_all[b], rounded, preferred_element_type=F32))
            acc[3] += fold(gradient * gradient)
            acc[4] += fold(step * step)
            acc[5] += fold(step * flat)
        for j in range(SIZE):
            b = p * SIZE + j
            image = made[j] + image_ref[index_ref[0, base + j]]
            image_ref[b] = image
            final = ends_ref[base + j]
            weighted = w_ref[...] * image
            acc[6] += final * fold(weighted * image)
            acc[7] += final * fold(weighted * s_ref[b])

    sweep(second_make, second_settle,
          [(LEAD - 1, lambda: reduce_middle(0)), (FAR + LATE, first_scalars)], LATE)

    reduce_start(1, (3, 4, 5, 6, 7))
    for s in range(1, cols):
        exchange(s).wait_send()

    @pl.when(has_near)
    def _():
        def drain(p, carry):
            back(p).wait_send()
            return carry

        lax.fori_loop(0, pieces, drain, 0)

    reduce_middle(1)
    total = reduce_end(1)
    alpha, gamma = scal[0:1], scal[2:3]
    flat, square = scal[3:4], scal[4:5]
    gamma_next = wide(total[0:1]) * share
    beta = gamma_next / gamma
    flat_next = wide(total[1:2]) * share + 2.0 * beta * wide(total[2:3]) * share + beta * beta * flat
    square_next = wide(total[3:4]) + 2.0 * beta * wide(total[4:5]) + beta * beta * square
    alpha_next = gamma_next / (square_next + ridge * flat_next)
    mixed = alpha + alpha_next * beta

    wide_part = t_ref.shape[1] // PARTS

    def leaving(k):
        place = pl.ds(k * wide_part, wide_part)
        return pltpu.make_async_copy(t_ref.at[:, place], residual_hbm.at[:, place], leave.at[k])

    for k in range(PARTS):
        def column(i, carry):
            c = k * (wide_part // BLOCK) + i
            place = pl.ds(pl.multiple_of(c * BLOCK, BLOCK), BLOCK)
            fitted = mixed * s_ref[last_ref[c]] + alpha_next * image_ref[last_ref[c]]
            t_ref[:, place] = (t_ref[:, place].astype(F32) - fitted).astype(BF16)
            return carry

        lax.fori_loop(0, wide_part // BLOCK, column, 0, unroll=2)
        leaving(k).start()

    runs = coeffs_ref.shape[0] // run
    for u in range(runs):
        slot = xor(my_col, my_row * runs + u, bits)

        def own(i, carry):
            b = slot * run + i
            coeffs_ref[u * run + i] = mixed * d_ref[b].astype(F32) + alpha_next * low_ref[b].astype(F32)
            return carry

        lax.fori_loop(0, run, own, 0)
    for k in range(PARTS):
        leaving(k).wait()


def fit(row_places, col_places, index, ends, last, times, x, targets, run, ridge, shard):
    cols, rows = lax.axis_size("col"), lax.axis_size("row")
    count = run * cols
    samples = x.shape[0]
    pieces = count // SIZE
    block = (BLOCK, BLOCK)
    dma = pltpu.SemaphoreType.DMA
    return pl.pallas_call(
        functools.partial(fit_kernel, run, ridge),
        out_shape=(
            jax.ShapeDtypeStruct(x.shape, BF16),
            jax.ShapeDtypeStruct((shard,) + block, F32),
        ),
        in_specs=[SCALARS] * 5 + [WHOLE, APART, APART],
        out_specs=(APART, WHOLE),
        scratch_shapes=[
            VMEM(x.shape, BF16), VMEM(x.shape, BF16), VMEM((samples, BLOCK), F32),
            VMEM((count + 1, samples, BLOCK), F32),
            VMEM((count, samples, BLOCK), BF16), VMEM((count, samples, BLOCK), BF16),
            VMEM((count,) + block, BF16), VMEM((count,) + block, BF16),
            VMEM((2, count) + block, BF16),
            VMEM((count,) + block, BF16), VMEM((count,) + block, BF16),
            VMEM((count + 1, samples, BLOCK), F32),
            VMEM((8, 8, LANES), F32), VMEM((8, LANES), F32),
            VMEM((2, 8, LANES), F32), VMEM((2, cols, 8, LANES), F32),
            VMEM((2, 8, LANES), F32), VMEM((2, rows, 8, LANES), F32),
            dma((cols - 1,)), dma((cols - 1,)),
            dma((2, pieces)), dma((2, pieces)),
            dma((2, cols - 1)), dma((2, cols - 1)),
            dma((2, rows - 1)), dma((2, rows - 1)),
            pltpu.SemaphoreType.REGULAR, dma((2,)), dma((PARTS,)),
        ],
        compiler_params=pltpu.CompilerParams(
            collective_id=2, has_side_effects=True, vmem_limit_bytes=66_000_000,
        ),
    )(row_places, col_places, index, ends, last, times, x, targets)


def on_device(samples_x, targets, times, block_rows, block_cols):
    col_count = lax.axis_size("col")
    row_count = lax.axis_size("row")
    taxa_col = samples_x.shape[1]
    sample_count = samples_x.shape[0]
    column_count = taxa_col // BLOCK
    my_col = lax.axis_index("col")
    shard = block_rows.shape[0]
    count = shard * row_count
    run = count // col_count
    ridge = RIDGE_SHARE * sample_count * row_count
    row_places, col_places = positions(block_rows, block_cols, column_count, 1)
    cols = col_places[:, :shard].reshape(count)

    number = lax.iota(jnp.int32, count)
    slot = jnp.bitwise_xor(lax.div(number, run), my_col) * run + lax.rem(number, run)
    same = cols[:, None] == cols[None, :]
    final = jnp.max(jnp.where(same, slot[None, :], -1), axis=1)
    before = jnp.max(jnp.where(same & (slot[None, :] < slot[:, None]), slot[None, :], -1), axis=1)
    before = jnp.where(before < 0, count, before)
    held = lax.iota(jnp.int32, column_count)[:, None] == cols[None, :]
    end = jnp.max(jnp.where(held, slot[None, :], -1), axis=1)
    end = jnp.where(end < 0, count, end)
    index = jnp.stack([before, final])

    ends = (final == slot).astype(F32)
    residual, coeffs = fit(row_places, col_places, index, ends, end, times[None], samples_x, targets, run, ridge, shard)
    return (coeffs, residual.astype(F32))


def solution(mesh):
    placed = (P("row", "col"), P("row", "col"), P("row"), P(("col", "row")), P(("col", "row")))
    return jax.shard_map(
        on_device,
        mesh=mesh,
        in_specs=placed,
        out_specs=(P(("col", "row"), None, None), P("row", "col")),
        check_vma=False,
    )
```
